32 devices in a mesh: mp: 2 (over y), survey: 16 (over z, x, core).
Axes of the slice: x: 2, y: 2, z: 4, core: 2. Of those that a mesh axis runs over, the one named last changes fastest.
Arguments:
- model: bfloat16 [64, 64, 128], P(('mp', 'survey')), may hold values from -6 to 6
- observed: bfloat16 [32, 64, 128], P(('mp', 'survey')), may hold values from -6 to 6
- weights: bfloat16 [32, 64, 128], P(('mp', 'survey')), may hold values from 0.29882812 to 3
- sensitivity: bfloat16 [2, 2048, 128, 128], P('mp', 'survey'), may hold values from -0.046875 to 0.046875
- block_rows: int32 [2, 2048], P('mp', 'survey'), may hold values from 0 to 15
- block_cols: int32 [2, 2048], P('mp', 'survey'), may hold values from 0 to 3
- block_count: int32 [2, 16], P('mp', 'survey'), may hold values from 32 to 128, as said below
Outputs:
- gradient: float32 [64, 64, 128], P(('mp', 'survey'))
The draws below stay inside these ranges and needn't reach their ends.
Inputs may be any that keep to these rules, and one draw needn't show every extreme that they name: `block_count`: some device uses all 128 slots.
All inputs are finite; a program needn't handle non-finite values.
Results may differ from the reference program's by a relative error of at most 0.0017.
Values may be sent and summed in bfloat16 or wider, within the bound.
A program may use at most 64 MiB of HBM per device.

```python
import math
import jax
import jax.numpy as jnp
from jax import lax

B = 128
NT = 64
KB = 128
MB_DEV = 2
DB_DEV = 1
DB = 16
SL = 4
NMB = 64
NDB = 32
N_MP = 2
N_SURVEY = 16


def draw_block_count(key, part):
    counts = jax.random.randint(key, (N_MP, N_SURVEY), KB // 4, KB + 1)
    spot = jax.random.randint(jax.random.fold_in(key, 7), (), 0, N_MP * N_SURVEY)
    flat_counts = counts.reshape(-1).at[spot].set(KB)
    return flat_counts.reshape(N_MP, N_SURVEY).astype(jnp.int32)


def touch_ends(entries, own_key, smallest, high):
    extent = entries.shape
    index_at = [jax.random.randint(jax.random.fold_in(own_key, axis), (), 0, extent[axis]) for axis in range(len(extent))]
    entries = entries.at[tuple(index_at)].set(smallest)
    longest = extent.index(max(extent))
    index_at[longest] = (index_at[longest] + 1) % extent[longest]
    return entries.at[tuple(index_at)].set(high)


def steps_of(stream_key, extent, pieces, least, largest):
    loudness, own = 1.0, jax.random.fold_in(stream_key, 6)
    for dim, shards_of in pieces:
        steps = jnp.exp(jax.random.uniform(jax.random.fold_in(own, dim), (shards_of,), jnp.float32, least / len(pieces), largest / len(pieces)))
        loudness = loudness * jnp.repeat(steps, extent[dim] // shards_of).reshape([-1 if axis == dim else 1 for axis in range(len(extent))])
    return loudness


def scatter_about(stream_key, extent, deviation, bound, cuts=(), kind=jnp.bfloat16):
    factor_of = steps_of(stream_key, extent, cuts, -0.22, 0.18) if cuts else 1.0
    drawn = jax.random.normal(stream_key, extent, jnp.float32) * deviation * factor_of
    return jnp.minimum(jnp.maximum(drawn, -bound), bound).astype(kind)


def setup_inputs(seed: int = 0) -> dict:
    keys = jax.random.split(jax.random.key(seed), 8)
    return {
        "model": scatter_about(keys[0], (NMB, NT, B), 1.0, 6.0, ((0, 32),)),
        "observed": scatter_about(keys[1], (NDB, NT, B), 1.0, 6.0, ((0, 32),)),
        "weights": jnp.clip(jnp.exp(math.log(3.0) - 2.306499 * jax.random.uniform(keys[2], (NDB, NT, B), jnp.float32) ** steps_of(keys[2], (NDB, NT, B), ((0, 32),), -0.2, 0.2)), 0.29882812, 3.0).astype(jnp.bfloat16),
        "sensitivity": scatter_about(keys[3], (N_MP, N_SURVEY * KB, B, B), (KB * B) ** -0.5, 0.046875, ((0, 2), (1, 16))),
        "block_rows": touch_ends(jax.random.randint(keys[4], (N_MP, N_SURVEY * KB), 0, DB), jax.random.fold_in(keys[4], 1), 0, DB - 1).astype(jnp.int32),
        "block_cols": touch_ends(jax.random.randint(keys[5], (N_MP, N_SURVEY * KB), 0, SL), jax.random.fold_in(keys[5], 1), 0, SL - 1).astype(jnp.int32),
        "block_count": draw_block_count(jax.random.fold_in(keys[7], 71), 0),
    }


SMOOTH = 0.5


def smoothing(model):
    field_f32 = model.astype(jnp.float32)
    earlier = jnp.concatenate([field_f32[:, :1], field_f32[:, :-1]], axis=1)
    later_step = jnp.concatenate([field_f32[:, 1:], field_f32[:, -1:]], axis=1)
    return SMOOTH * (2.0 * field_f32 - earlier - later_step)


def reference(model, observed, weights, sensitivity, block_rows, block_cols, block_count):
    group_rows = DB_DEV * N_SURVEY
    slab_rows = MB_DEV * N_MP
    slabs = jnp.transpose(model.reshape(N_MP, N_SURVEY, MB_DEV, NT, B), (1, 0, 2, 3, 4)).reshape(N_SURVEY, slab_rows, NT, B)
    in_use_all = jnp.arange(KB, dtype=jnp.int32)[None, None, :] < block_count[:, :, None]
    row_ids_all = block_rows.reshape(N_MP, N_SURVEY, KB)
    col_ids_all = block_cols.reshape(N_MP, N_SURVEY, KB)
    blocks_all = sensitivity.reshape(N_MP, N_SURVEY, KB, B, B)
    seen_all = observed.reshape(N_MP, group_rows, NT, B)
    weight_all = weights.reshape(N_MP, group_rows, NT, B)
    survey_ids = jnp.arange(N_SURVEY, dtype=jnp.int32)[:, None]

    def one_group(running, group_item):
        blocks, row_ids, col_ids, in_use, seen_data, data_weight = group_item
        picked = slabs[survey_ids, col_ids]
        terms = jnp.einsum('sktc,skrc->sktr', picked.astype(jnp.float32), blocks.astype(jnp.float32))
        terms = jnp.where(in_use[:, :, None, None], terms, 0.0)
        predicted = jax.ops.segment_sum(terms.reshape(N_SURVEY * KB, NT, B), row_ids.reshape(-1), num_segments=group_rows)
        residual = (data_weight.astype(jnp.float32) * (predicted - seen_data.astype(jnp.float32))).astype(jnp.bfloat16)
        resid_rows = residual[row_ids]
        back_terms = jnp.einsum('sktr,skrc->sktc', resid_rows.astype(jnp.float32), blocks.astype(jnp.float32))
        back_terms = jnp.where(in_use[:, :, None, None], back_terms, 0.0)
        flat_ids = (survey_ids * slab_rows + col_ids).reshape(-1).astype(jnp.int32)
        gradient_slab = jax.ops.segment_sum(back_terms.reshape(N_SURVEY * KB, NT, B), flat_ids, num_segments=N_SURVEY * slab_rows)
        return running + gradient_slab.reshape(N_SURVEY, slab_rows, NT, B), None

    start_sum = jnp.zeros((N_SURVEY, slab_rows, NT, B), jnp.float32)
    summed, _ = lax.scan(one_group, start_sum, (blocks_all, row_ids_all, col_ids_all, in_use_all, seen_all, weight_all))
    misfit_gradient = jnp.transpose(summed.reshape(N_SURVEY, N_MP, MB_DEV, NT, B), (1, 0, 2, 3, 4)).reshape(N_MP * N_SURVEY * MB_DEV, NT, B)
    return misfit_gradient + smoothing(model)
```

```python
import functools

import jax
import jax.numpy as jnp
from jax import lax
from jax.experimental import pallas as pl
from jax.experimental.pallas import tpu as pltpu
from jax.sharding import PartitionSpec as P

SMOOTH = 0.5
MESH = pl.DeviceIdType.MESH
PARTS = 8
UNROLL = 8


def smoothing(field):
    steps = field.shape[0]
    at = lax.broadcasted_iota(jnp.int32, field.shape, 0)
    earlier = jnp.where(at == 0, field, pltpu.roll(field, 1, 0))
    later_step = jnp.where(at == steps - 1, field, pltpu.roll(field, steps - 1, 0))
    return SMOOTH * (2.0 * field - earlier - later_step)


def kernel(
    n_mp,
    n_survey,
    rows_ref,
    cols_ref,
    row_links,
    col_links,
    model_ref,
    seen_ref,
    weight_ref,
    sens_hbm,
    out_ref,
    blocks,
    slab,
    chain,
    sib_send,
    sib_recv,
    chip_send,
    chip_recv,
    resid,
    grad_send,
    grad_recv,
    load_sem,
    model_sem,
    sib_sem,
    chip_sem,
    own_sem,
    gather_sem,
    relay_sem,
    grad_sem,
):
    m = lax.axis_index("mp")
    s = lax.axis_index("survey")
    chips = n_survey // 2
    chip, core = s // 2, s % 2
    sibling = (m, chip * 2 + 1 - core)
    slots = blocks.shape[0]
    owned = model_ref.shape[0]
    per = seen_ref.shape[0]

    def chip_at(j):
        return (chip + j) % chips

    def copy(src, dst, sems, j, device):
        return pltpu.make_async_remote_copy(
            src_ref=src,
            dst_ref=dst,
            send_sem=sems.at[0, j],
            recv_sem=sems.at[1, j],
            device_id=device,
            device_id_type=MESH,
        )

    step = slots // PARTS
    loads = [
        pltpu.make_async_copy(
            sens_hbm.at[pl.ds(i * step, step)], blocks.at[pl.ds(i * step, step)], load_sem.at[i]
        )
        for i in range(PARTS)
    ]
    for load in loads:
        load.start()

    barrier = pltpu.get_barrier_semaphore()
    partners = [((m + j) % n_mp, s) for j in range(1, n_mp)] + [sibling]
    partners += [(m, chip_at(j) * 2 + core) for j in range(1, chips)]
    for partner in partners:
        pl.semaphore_signal(barrier, inc=1, device_id=partner, device_id_type=MESH)
    pl.semaphore_wait(barrier, len(partners))

    here = pl.ds(m * owned, owned)
    sends = [
        copy(model_ref, slab.at[here], model_sem, j - 1, ((m + j) % n_mp, s))
        for j in range(1, n_mp)
    ]
    for send in sends:
        send.start()
    slab[here] = model_ref[...]
    for i in range(owned):
        out_ref[i] = smoothing(model_ref[i].astype(jnp.float32))
    chain[0] = jnp.zeros(chain.shape[1:], jnp.float32)
    for load in loads:
        load.wait()
    for send in sends:
        send.wait()

    def forward(g, carry):
        base = g * UNROLL
        terms = [
            lax.dot_general(
                slab[cols_ref[base + u]],
                blocks[base + u],
                (((1,), (1,)), ((), ())),
                preferred_element_type=jnp.float32,
            )
            for u in range(UNROLL)
        ]
        for u in range(UNROLL):
            chain[base + u + 1] = terms[u] + chain[row_links[base + u]]
        return carry

    lax.fori_loop(0, slots // UNROLL, forward, 0)

    order = list(range(1, chips)) + [0]
    swaps = {}
    for j in order:
        for i in range(per):
            sib_send[j, i] = chain[row_links[slots + (chip_at(j) * 2 + 1 - core) * per + i]]
        swaps[j] = copy(sib_send.at[j], sib_recv.at[j], sib_sem, j, sibling)
        swaps[j].start()
    scatters = {}
    for j in order:
        swaps[j].wait_recv()
        for i in range(per):
            mine = chain[row_links[slots + (chip_at(j) * 2 + core) * per + i]]
            chip_send[j, i] = mine + sib_recv[j, i]
        if j:
            scatters[j] = copy(
                chip_send.at[j], chip_recv.at[j], chip_sem, j, (m, chip_at(j) * 2 + core)
            )
            scatters[j].start()
    total = chip_send[0]
    for j in range(1, chips):
        scatters[j].wait_recv()
        total += chip_recv[j]

    value = weight_ref[...].astype(jnp.float32) * (total - seen_ref[...].astype(jnp.float32))
    mine = resid.at[pl.ds(s * per, per)]
    resid[pl.ds(s * per, per)] = value.astype(jnp.bfloat16)
    gathers = {}
    for j in range(1, chips):
        gathers[j] = copy(mine, mine, gather_sem, j, (m, chip_at(j) * 2 + core))
        gathers[j].start()
    own = copy(mine, mine, own_sem, 0, sibling)
    own.start()
    relays = {}
    for j in range(1, chips):
        gathers[j].wait_recv()
        source = resid.at[pl.ds((chip_at(chips - j) * 2 + core) * per, per)]
        relays[j] = copy(source, source, relay_sem, j, sibling)
        relays[j].start()
    own.wait_recv()
    for j in range(1, chips):
        relays[j].wait_recv()

    def backward(g, carry):
        base = g * UNROLL
        terms = [
            jnp.dot(
                resid[rows_ref[base + u]], blocks[base + u], preferred_element_type=jnp.float32
            )
            for u in range(UNROLL)
        ]
        for u in range(UNROLL):
            chain[base + u + 1] = terms[u] + chain[col_links[base + u]]
        return carry

    lax.fori_loop(0, slots // UNROLL, backward, 0)

    returns = {}
    for j in range(1, n_mp):
        owner = (m + j) % n_mp
        for i in range(owned):
            grad_send[j, i] = chain[col_links[slots + owner * owned + i]]
        returns[j] = copy(grad_send.at[j], grad_recv.at[j], grad_sem, j, (owner, s))
        returns[j].start()
    for i in range(owned):
        out_ref[i] += chain[col_links[slots + m * owned + i]]
    for j in range(1, n_mp):
        returns[j].wait_recv()
        out_ref[...] += grad_recv[j]

    own.wait_send()
    for group in (swaps, scatters, gathers, relays, returns):
        for sent in group.values():
            sent.wait_send()


def links(ids, in_use, count):
    slots = ids.shape[0]
    at = jnp.arange(slots, dtype=jnp.int32)
    wanted = jnp.concatenate([ids, jnp.arange(count, dtype=jnp.int32)])
    limit = jnp.concatenate([at, jnp.full((count,), slots, jnp.int32)])
    hit = (wanted[:, None] == ids[None, :]) & (at[None, :] < limit[:, None]) & in_use[None, :]
    return jnp.max(jnp.where(hit, at[None, :] + 1, 0), axis=1)


def on_device(
    n_mp, n_survey, model, observed, weights, sensitivity, block_rows, block_cols, block_count
):
    row_ids, col_ids = block_rows[0], block_cols[0]
    slots = row_ids.shape[0]
    owned, steps, cells = model.shape
    per = observed.shape[0]
    chips = n_survey // 2
    in_use = jnp.arange(slots, dtype=jnp.int32) < block_count[0, 0]
    row_links = links(row_ids, in_use, per * n_survey)
    col_links = links(col_ids, in_use, owned * n_mp)
    smem = pl.BlockSpec(memory_space=pltpu.SMEM)
    vmem = pl.BlockSpec(memory_space=pltpu.VMEM)
    pair = lambda n: pltpu.SemaphoreType.DMA((2, n))
    f32, bf16 = jnp.float32, jnp.bfloat16
    return pl.pallas_call(
        functools.partial(kernel, n_mp, n_survey),
        out_shape=jax.ShapeDtypeStruct(model.shape, f32),
        in_specs=[smem] * 4 + [vmem] * 3 + [pl.BlockSpec(memory_space=pl.ANY)],
        out_specs=vmem,
        scratch_shapes=[
            pltpu.VMEM(sensitivity.shape[1:], bf16),
            pltpu.VMEM((owned * n_mp, steps, cells), bf16),
            pltpu.VMEM((slots + 1, steps, cells), f32),
            pltpu.VMEM((chips, per, steps, cells), f32),
            pltpu.VMEM((chips, per, steps, cells), f32),
            pltpu.VMEM((chips, per, steps, cells), f32),
            pltpu.VMEM((chips, per, steps, cells), f32),
            pltpu.VMEM((per * n_survey, steps, cells), bf16),
            pltpu.VMEM((n_mp, owned, steps, cells), f32),
            pltpu.VMEM((n_mp, owned, steps, cells), f32),
            pltpu.SemaphoreType.DMA((PARTS,)),
            pair(n_mp),
            pair(chips),
            pair(chips),
            pair(1),
            pair(chips),
            pair(chips),
            pair(n_mp),
        ],
        compiler_params=pltpu.CompilerParams(
            collective_id=0, has_side_effects=True, vmem_limit_bytes=40 << 20
        ),
    )(row_ids, col_ids, row_links, col_links, model, observed, weights, sensitivity[0])


def solution(mesh):
    n_mp, n_survey = mesh.shape["mp"], mesh.shape["survey"]
    in_specs = (
        P(("mp", "survey"), None, None),
        P(("mp", "survey"), None, None),
        P(("mp", "survey"), None, None),
        P("mp", "survey", None, None),
        P("mp", "survey"),
        P("mp", "survey"),
        P("mp", "survey"),
    )
    out_specs = P(("mp", "survey"), None, None)
    return jax.shard_map(
        functools.partial(on_device, n_mp, n_survey),
        mesh=mesh,
        in_specs=in_specs,
        out_specs=out_specs,
        check_vma=False,
    )
```

```python
import functools

import jax
import jax.numpy as jnp
from jax import lax
from jax.experimental import pallas as pl
from jax.experimental.pallas import tpu as pltpu
from jax.sharding import PartitionSpec as P

SMOOTH = 0.5
MESH = pl.DeviceIdType.MESH
PARTS = 8
UNROLL = 8


def smoothing(field):
    steps = field.shape[0]
    at = lax.broadcasted_iota(jnp.int32, field.shape, 0)
    earlier = jnp.where(at == 0, field, pltpu.roll(field, 1, 0))
    later_step = jnp.where(at == steps - 1, field, pltpu.roll(field, steps - 1, 0))
    return SMOOTH * (2.0 * field - earlier - later_step)


def link_tables(ids, count):
    slots = ids.shape[1]
    wide = jnp.broadcast_to(ids, (slots, slots))
    tall = wide.T
    j = lax.broadcasted_iota(jnp.int32, (slots, slots), 0)
    q = lax.broadcasted_iota(jnp.int32, (slots, slots), 1)
    at = jnp.where(j < count, j + 1, 0)
    before = jnp.max(jnp.where((tall == wide) & (j < q), at, 0), axis=0, keepdims=True)
    last = jnp.max(jnp.where(tall == q, at, 0), axis=0, keepdims=True)
    return before, last


ROW, ROW_BEFORE, ROW_LAST, COL, COL_BEFORE, COL_LAST = range(6)


def kernel(
    n_mp,
    n_survey,
    rows_hbm,
    cols_hbm,
    count_hbm,
    model_hbm,
    seen_hbm,
    weight_hbm,
    sens_hbm,
    out_ref,
    blocks,
    slab,
    chain,
    sib_send,
    sib_recv,
    chip_send,
    chip_recv,
    resid,
    grad_send,
    grad_recv,
    model_ref,
    seen_ref,
    weight_ref,
    ids_ref,
    count_ref,
    tables,
    table,
    load_sem,
    small_sem,
    model_sem,
    sib_sem,
    chip_sem,
    own_sem,
    gather_sem,
    relay_sem,
    grad_sem,
):
    m = lax.axis_index("mp")
    s = lax.axis_index("survey")
    chips = n_survey // 2
    chip, core = s // 2, s % 2
    sibling = (m, chip * 2 + 1 - core)
    slots = blocks.shape[0]
    owned = model_ref.shape[0]
    per = seen_ref.shape[0]

    def chip_at(j):
        return (chip + j) % chips

    def copy(src, dst, sems, j, device):
        return pltpu.make_async_remote_copy(
            src_ref=src,
            dst_ref=dst,
            send_sem=sems.at[0, j],
            recv_sem=sems.at[1, j],
            device_id=device,
            device_id_type=MESH,
        )

    smalls = [
        pltpu.make_async_copy(src, dst, small_sem.at[i])
        for i, (src, dst) in enumerate(
            (
                (count_hbm, count_ref),
                (rows_hbm, ids_ref.at[0]),
                (cols_hbm, ids_ref.at[1]),
                (model_hbm, model_ref),
                (seen_hbm, seen_ref),
                (weight_hbm, weight_ref),
            )
        )
    ]
    step = slots // PARTS
    loads = [
        pltpu.make_async_copy(
            sens_hbm.at[0, pl.ds(i * step, step)], blocks.at[pl.ds(i * step, step)], load_sem.at[i]
        )
        for i in range(PARTS)
    ]

    barrier = pltpu.get_barrier_semaphore()
    partners = [((m + j) % n_mp, s) for j in range(1, n_mp)] + [sibling]
    partners += [(m, chip_at(j) * 2 + core) for j in range(1, chips)]
    for partner in partners:
        pl.semaphore_signal(barrier, inc=1, device_id=partner, device_id_type=MESH)
    for load in smalls + loads:
        load.start()

    for small in smalls[:3]:
        small.wait()
    count = count_ref[0, 0]
    for base, which in ((ROW, 0), (COL, 1)):
        ids = ids_ref[which]
        before, last = link_tables(ids, count)
        tables[pl.ds(base, 1)] = ids
        tables[pl.ds(base + 1, 1)] = before
        tables[pl.ds(base + 2, 1)] = last
    to_scalars = pltpu.make_async_copy(tables, table, small_sem.at[6])
    to_scalars.start()
    pl.semaphore_wait(barrier, len(partners))

    here = pl.ds(m * owned, owned)
    sends = [
        copy(model_hbm, slab.at[here], model_sem, j - 1, ((m + j) % n_mp, s))
        for j in range(1, n_mp)
    ]
    for send in sends:
        send.start()
    smalls[3].wait()
    slab[here] = model_ref[...]
    for i in range(owned):
        out_ref[i] = smoothing(model_ref[i].astype(jnp.float32))
    chain[0] = jnp.zeros(chain.shape[1:], jnp.float32)
    for load in loads + [to_scalars] + smalls[4:]:
        load.wait()
    for send in sends:
        send.wait()

    def forward(g, carry):
        base = g * UNROLL
        terms = [
            lax.dot_general(
                slab[table[COL, base + u]],
                blocks[base + u],
                (((1,), (1,)), ((), ())),
                preferred_element_type=jnp.float32,
            )
            for u in range(UNROLL)
        ]
        for u in range(UNROLL):
            chain[base + u + 1] = terms[u] + chain[table[ROW_BEFORE, base + u]]
        return carry

    lax.fori_loop(0, slots // UNROLL, forward, 0)

    order = list(range(1, chips)) + [0]
    swaps = {}
    for j in order:
        for i in range(per):
            sib_send[j, i] = chain[table[ROW_LAST, (chip_at(j) * 2 + 1 - core) * per + i]]
        swaps[j] = copy(sib_send.at[j], sib_recv.at[j], sib_sem, j, sibling)
        swaps[j].start()
    scatters = {}
    for j in order:
        swaps[j].wait_recv()
        for i in range(per):
            mine = chain[table[ROW_LAST, (chip_at(j) * 2 + core) * per + i]]
            chip_send[j, i] = mine + sib_recv[j, i]
        if j:
            scatters[j] = copy(
                chip_send.at[j], chip_recv.at[j], chip_sem, j, (m, chip_at(j) * 2 + core)
            )
            scatters[j].start()
    total = chip_send[0]
    for j in range(1, chips):
        scatters[j].wait_recv()
        total += chip_recv[j]

    value = weight_ref[...].astype(jnp.float32) * (total - seen_ref[...].astype(jnp.float32))
    mine = resid.at[pl.ds(s * per, per)]
    resid[pl.ds(s * per, per)] = value.astype(jnp.bfloat16)
    gathers = {}
    for j in range(1, chips):
        gathers[j] = copy(mine, mine, gather_sem, j, (m, chip_at(j) * 2 + core))
        gathers[j].start()
    own = copy(mine, mine, own_sem, 0, sibling)
    own.start()
    relays = {}
    for j in range(1, chips):
        gathers[j].wait_recv()
        source = resid.at[pl.ds((chip_at(chips - j) * 2 + core) * per, per)]
        relays[j] = copy(source, source, relay_sem, j, sibling)
        relays[j].start()
    own.wait_recv()
    for j in range(1, chips):
        relays[j].wait_recv()

    def backward(g, carry):
        base = g * UNROLL
        terms = [
            jnp.dot(
                resid[table[ROW, base + u]], blocks[base + u], preferred_element_type=jnp.float32
            )
            for u in range(UNROLL)
        ]
        for u in range(UNROLL):
            chain[base + u + 1] = terms[u] + chain[table[COL_BEFORE, base + u]]
        return carry

    lax.fori_loop(0, slots // UNROLL, backward, 0)

    returns = {}
    for j in range(1, n_mp):
        owner = (m + j) % n_mp
        for i in range(owned):
            grad_send[j, i] = chain[table[COL_LAST, owner * owned + i]]
        returns[j] = copy(grad_send.at[j], grad_recv.at[j], grad_sem, j, (owner, s))
        returns[j].start()
    for i in range(owned):
        out_ref[i] += chain[table[COL_LAST, m * owned + i]]
    for j in range(1, n_mp):
        returns[j].wait_recv()
        out_ref[...] += grad_recv[j]

    own.wait_send()
    for group in (swaps, scatters, gathers, relays, returns):
        for sent in group.values():
            sent.wait_send()


def on_device(
    n_mp, n_survey, model, observed, weights, sensitivity, block_rows, block_cols, block_count
):
    slots = block_rows.shape[1]
    owned, steps, cells = model.shape
    per = observed.shape[0]
    chips = n_survey // 2
    pair = lambda n: pltpu.SemaphoreType.DMA((2, n))
    f32, bf16, i32 = jnp.float32, jnp.bfloat16, jnp.int32
    return pl.pallas_call(
        functools.partial(kernel, n_mp, n_survey),
        out_shape=jax.ShapeDtypeStruct(model.shape, f32),
        in_specs=[pl.BlockSpec(memory_space=pl.ANY)] * 7,
        out_specs=pl.BlockSpec(memory_space=pltpu.VMEM),
        scratch_shapes=[
            pltpu.VMEM(sensitivity.shape[1:], bf16),
            pltpu.VMEM((owned * n_mp, steps, cells), bf16),
            pltpu.VMEM((slots + 1, steps, cells), f32),
            pltpu.VMEM((chips, per, steps, cells), f32),
            pltpu.VMEM((chips, per, steps, cells), f32),
            pltpu.VMEM((chips, per, steps, cells), f32),
            pltpu.VMEM((chips, per, steps, cells), f32),
            pltpu.VMEM((per * n_survey, steps, cells), bf16),
            pltpu.VMEM((n_mp, owned, steps, cells), f32),
            pltpu.VMEM((n_mp, owned, steps, cells), f32),
            pltpu.VMEM(model.shape, bf16),
            pltpu.VMEM(observed.shape, bf16),
            pltpu.VMEM(weights.shape, bf16),
            pltpu.VMEM((2, 1, slots), i32),
            pltpu.SMEM((1, 1), i32),
            pltpu.VMEM((8, slots), i32),
            pltpu.SMEM((8, slots), i32),
            pltpu.SemaphoreType.DMA((PARTS,)),
            pltpu.SemaphoreType.DMA((7,)),
            pair(n_mp),
            pair(chips),
            pair(chips),
            pair(1),
            pair(chips),
            pair(chips),
            pair(n_mp),
        ],
        compiler_params=pltpu.CompilerParams(
            collective_id=0, has_side_effects=True, vmem_limit_bytes=60 << 20
        ),
    )(block_rows, block_cols, block_count, model, observed, weights, sensitivity)


def solution(mesh):
    n_mp, n_survey = mesh.shape["mp"], mesh.shape["survey"]
    in_specs = (
        P(("mp", "survey"), None, None),
        P(("mp", "survey"), None, None),
        P(("mp", "survey"), None, None),
        P("mp", "survey", None, None),
        P("mp", "survey"),
        P("mp", "survey"),
        P("mp", "survey"),
    )
    out_specs = P(("mp", "survey"), None, None)
    return jax.shard_map(
        functools.partial(on_device, n_mp, n_survey),
        mesh=mesh,
        in_specs=in_specs,
        out_specs=out_specs,
        check_vma=False,
    )
```

```python
import functools

import jax
import jax.numpy as jnp
from jax import lax
from jax.experimental import pallas as pl
from jax.experimental.pallas import tpu as pltpu
from jax.sharding import PartitionSpec as P

SMOOTH = 0.5
MESH = pl.DeviceIdType.MESH
PARTS = 8
UNROLL = 64
SWAPS = 2


def smoothing(field):
    steps = field.shape[0]
    at = lax.broadcasted_iota(jnp.int32, field.shape, 0)
    earlier = jnp.where(at == 0, field, pltpu.roll(field, 1, 0))
    later_step = jnp.where(at == steps - 1, field, pltpu.roll(field, steps - 1, 0))
    return SMOOTH * (2.0 * field - earlier - later_step)


def link_tables(ids, count):
    slots = ids.shape[1]
    wide = jnp.broadcast_to(ids, (slots, slots))
    tall = wide.T
    j = lax.broadcasted_iota(jnp.int32, (slots, slots), 0)
    q = lax.broadcasted_iota(jnp.int32, (slots, slots), 1)
    at = jnp.where(j < count, j + 1, 0)
    before = jnp.max(jnp.where((tall == wide) & (j < q), at, 0), axis=0, keepdims=True)
    last = jnp.max(jnp.where(tall == q, at, 0), axis=0, keepdims=True)
    return before, last


ROW, ROW_BEFORE, ROW_LAST, COL, COL_BEFORE, COL_LAST = range(6)


def kernel(
    n_mp,
    n_survey,
    rows_hbm,
    cols_hbm,
    count_hbm,
    model_hbm,
    seen_hbm,
    weight_hbm,
    sens_hbm,
    out_ref,
    blocks,
    slab,
    chain,
    sib_send,
    sib_recv,
    chip_send,
    chip_recv,
    resid,
    grad_send,
    grad_recv,
    model_ref,
    seen_ref,
    weight_ref,
    ids_ref,
    count_ref,
    tables,
    table,
    load_sem,
    small_sem,
    model_sem,
    sib_sem,
    chip_sem,
    gather_sem,
    relay_sem,
    grad_sem,
):
    m = lax.axis_index("mp")
    s = lax.axis_index("survey")
    chips = n_survey // 2
    chip, core = s // 2, s % 2
    sibling = (m, chip * 2 + 1 - core)
    slots = blocks.shape[0]
    owned = model_ref.shape[0]
    per = seen_ref.shape[0]

    def chip_at(j):
        return (chip + j) % chips

    def copy(src, dst, sems, j, device):
        return pltpu.make_async_remote_copy(
            src_ref=src,
            dst_ref=dst,
            send_sem=sems.at[0, j],
            recv_sem=sems.at[1, j],
            device_id=device,
            device_id_type=MESH,
        )

    smalls = [
        pltpu.make_async_copy(src, dst, small_sem.at[i])
        for i, (src, dst) in enumerate(
            (
                (count_hbm, count_ref),
                (rows_hbm, ids_ref.at[0]),
                (cols_hbm, ids_ref.at[1]),
                (model_hbm, model_ref),
                (seen_hbm, seen_ref),
                (weight_hbm, weight_ref),
            )
        )
    ]
    part = slots // PARTS
    loads = [
        pltpu.make_async_copy(
            sens_hbm.at[0, pl.ds(i * part, part)], blocks.at[pl.ds(i * part, part)], load_sem.at[i]
        )
        for i in range(PARTS)
    ]

    barrier = pltpu.get_barrier_semaphore()
    partners = [((m + j) % n_mp, s) for j in range(1, n_mp)] + [sibling]
    partners += [(m, chip_at(j) * 2 + core) for j in range(1, chips)]
    for partner in partners:
        pl.semaphore_signal(barrier, inc=1, device_id=partner, device_id_type=MESH)
    for load in smalls + loads:
        load.start()

    for small in smalls[:3]:
        small.wait()
    count = count_ref[0, 0]
    for base, which in ((ROW, 0), (COL, 1)):
        ids = ids_ref[which]
        if base == ROW:
            owner = ids // per
            ids = (owner % 2 * chips + owner // 2) * per + ids % per
        before, last = link_tables(ids, count)
        tables[pl.ds(base, 1)] = ids
        tables[pl.ds(base + 1, 1)] = before
        tables[pl.ds(base + 2, 1)] = last
    to_scalars = pltpu.make_async_copy(tables, table, small_sem.at[6])
    to_scalars.start()
    pl.semaphore_wait(barrier, len(partners))

    here = pl.ds(m * owned, owned)
    sends = [
        copy(model_hbm, slab.at[here], model_sem, j - 1, ((m + j) % n_mp, s))
        for j in range(1, n_mp)
    ]
    for send in sends:
        send.start()
    smalls[3].wait()
    slab[here] = model_ref[...]
    for i in range(owned):
        out_ref[i] = smoothing(model_ref[i].astype(jnp.float32))
    chain[0] = jnp.zeros(chain.shape[1:], jnp.float32)
    for load in loads + [to_scalars] + smalls[4:]:
        load.wait()
    for send in sends:
        send.wait()

    def forward():
        def body(g, carry):
            base = g * UNROLL
            terms = [
                lax.dot_general(
                    slab[table[COL, base + u]],
                    blocks[base + u],
                    (((1,), (1,)), ((), ())),
                    preferred_element_type=jnp.float32,
                )
                for u in range(UNROLL)
            ]
            for u in range(UNROLL):
                before = chain[table[ROW_BEFORE, base + u]]
                chain[base + u + 1] = terms[u] + before
            return carry

        lax.fori_loop(0, slots // UNROLL, body, 0)

    def backward():
        def body(g, carry):
            base = g * UNROLL
            terms = [
                jnp.dot(
                    resid[table[ROW, base + u]],
                    blocks[base + u],
                    preferred_element_type=jnp.float32,
                )
                for u in range(UNROLL)
            ]
            for u in range(UNROLL):
                before = chain[table[COL_BEFORE, base + u]]
                chain[base + u + 1] = terms[u] + before
            return carry

        lax.fori_loop(0, slots // UNROLL, body, 0)

    forward()

    order = list(range(1, chips)) + [0]
    group = chips // SWAPS
    swaps, scatters, gathers, returns = {}, {}, {}, {}
    for p, j in enumerate(order):
        for i in range(per):
            row = ((1 - core) * chips + chip_at(j)) * per + i
            sib_send[p, i] = chain[table[ROW_LAST, row]]
        if (p + 1) % group == 0:
            some = pl.ds(p + 1 - group, group)
            swaps[p] = copy(sib_send.at[some], sib_recv.at[some], sib_sem, p, sibling)
            swaps[p].start()
    for p, j in enumerate(order):
        if p % group == 0:
            swaps[p + group - 1].wait_recv()
        for i in range(per):
            row = (core * chips + chip_at(j)) * per + i
            chip_send[j, i] = chain[table[ROW_LAST, row]] + sib_recv[p, i]
        if j:
            scatters[j] = copy(
                chip_send.at[j], chip_recv.at[j], chip_sem, j, (m, chip_at(j) * 2 + core)
            )
            scatters[j].start()

    total = chip_send[0]
    for j in range(1, chips):
        scatters[j].wait_recv()
        total += chip_recv[j]
    value = weight_ref[...].astype(jnp.float32) * (total - seen_ref[...].astype(jnp.float32))
    here = pl.ds((core * chips + chip) * per, per)
    resid[here] = value.astype(jnp.bfloat16)
    for j in range(1, chips):
        gathers[j] = copy(
            resid.at[here], resid.at[here], gather_sem, j, (m, chip_at(j) * 2 + core)
        )
        gathers[j].start()
    for j in range(1, chips):
        gathers[j].wait_recv()
    same = resid.at[pl.ds(core * chips * per, chips * per)]
    relay = copy(same, same, relay_sem, 0, sibling)
    relay.start()
    relay.wait_recv()

    backward()

    for j in range(1, n_mp):
        owner = (m + j) % n_mp
        for i in range(owned):
            grad_send[j, i] = chain[table[COL_LAST, owner * owned + i]]
        returns[j] = copy(grad_send.at[j], grad_recv.at[j], grad_sem, j, (owner, s))
        returns[j].start()
    for i in range(owned):
        out_ref[i] += chain[table[COL_LAST, m * owned + i]]
    for j in range(1, n_mp):
        returns[j].wait_recv()
        out_ref[...] += grad_recv[j]

    relay.wait_send()
    for sent in (swaps, scatters, gathers, returns):
        for one in sent.values():
            one.wait_send()


def on_device(
    n_mp, n_survey, model, observed, weights, sensitivity, block_rows, block_cols, block_count
):
    slots = block_rows.shape[1]
    owned, steps, cells = model.shape
    per = observed.shape[0]
    chips = n_survey // 2
    pair = lambda n: pltpu.SemaphoreType.DMA((2, n))
    f32, bf16, i32 = jnp.float32, jnp.bfloat16, jnp.int32
    return pl.pallas_call(
        functools.partial(kernel, n_mp, n_survey),
        out_shape=jax.ShapeDtypeStruct(model.shape, f32),
        in_specs=[pl.BlockSpec(memory_space=pl.ANY)] * 7,
        out_specs=pl.BlockSpec(memory_space=pltpu.VMEM),
        scratch_shapes=[
            pltpu.VMEM(sensitivity.shape[1:], bf16),
            pltpu.VMEM((owned * n_mp, steps, cells), bf16),
            pltpu.VMEM((slots + 1, steps, cells), f32),
            pltpu.VMEM((chips, per, steps, cells), f32),
            pltpu.VMEM((chips, per, steps, cells), f32),
            pltpu.VMEM((chips, per, steps, cells), f32),
            pltpu.VMEM((chips, per, steps, cells), f32),
            pltpu.VMEM((per * n_survey, steps, cells), bf16),
            pltpu.VMEM((n_mp, owned, steps, cells), f32),
            pltpu.VMEM((n_mp, owned, steps, cells), f32),
            pltpu.VMEM(model.shape, bf16),
            pltpu.VMEM(observed.shape, bf16),
            pltpu.VMEM(weights.shape, bf16),
            pltpu.VMEM((2, 1, slots), i32),
            pltpu.SMEM((1, 1), i32),
            pltpu.VMEM((8, slots), i32),
            pltpu.SMEM((8, slots), i32),
            pltpu.SemaphoreType.DMA((PARTS,)),
            pltpu.SemaphoreType.DMA((7,)),
            pair(n_mp),
            pair(chips),
            pair(chips),
            pair(chips),
            pair(chips),
            pair(n_mp),
        ],
        compiler_params=pltpu.CompilerParams(
            collective_id=0, has_side_effects=True, vmem_limit_bytes=60 << 20
        ),
    )(block_rows, block_cols, block_count, model, observed, weights, sensitivity)


def solution(mesh):
    n_mp, n_survey = mesh.shape["mp"], mesh.shape["survey"]
    in_specs = (
        P(("mp", "survey"), None, None),
        P(("mp", "survey"), None, None),
        P(("mp", "survey"), None, None),
        P("mp", "survey", None, None),
        P("mp", "survey"),
        P("mp", "survey"),
        P("mp", "survey"),
    )
    out_specs = P(("mp", "survey"), None, None)
    return jax.shard_map(
        functools.partial(on_device, n_mp, n_survey),
        mesh=mesh,
        in_specs=in_specs,
        out_specs=out_specs,
        check_vma=False,
    )
```

```python
import functools

import jax
import jax.numpy as jnp
from jax import lax
from jax.experimental import pallas as pl
from jax.experimental.pallas import tpu as pltpu
from jax.sharding import PartitionSpec as P

SMOOTH = 0.5
MESH = pl.DeviceIdType.MESH
PARTS = 8
UNROLL = 64
SWAPS = 2
LIMIT = 32


def smoothing(field):
    steps = field.shape[0]
    at = lax.broadcasted_iota(jnp.int32, field.shape, 0)
    earlier = jnp.where(at == 0, field, pltpu.roll(field, 1, 0))
    later_step = jnp.where(at == steps - 1, field, pltpu.roll(field, steps - 1, 0))
    return SMOOTH * (2.0 * field - earlier - later_step)


def link_tables(ids, count):
    slots = ids.shape[1]
    wide = jnp.broadcast_to(ids, (slots, slots))
    tall = wide.T
    j = lax.broadcasted_iota(jnp.int32, (slots, slots), 0)
    q = lax.broadcasted_iota(jnp.int32, (slots, slots), 1)
    at = jnp.where(j < count, j + 1, 0)
    before = jnp.max(jnp.where((tall == wide) & (j < q), at, 0), axis=0, keepdims=True)
    last = jnp.max(jnp.where(tall == q, at, 0), axis=0, keepdims=True)
    return before, last


ROW, ROW_BEFORE, ROW_LAST, COL, COL_BEFORE, COL_LAST = range(6)


def copy(src, dst, sems, j, device):
    return pltpu.make_async_remote_copy(
        src_ref=src,
        dst_ref=dst,
        send_sem=sems.at[0, j],
        recv_sem=sems.at[1, j],
        device_id=device,
        device_id_type=MESH,
    )


def collect(
    n_mp, n_survey, per, rows_hbm, cols_hbm, count_hbm, model_hbm, sens_hbm,
    table, slab, blocks, ids_ref, count_ref, tables, load_sem, small_sem, model_sem,
):
    m = lax.axis_index("mp")
    s = lax.axis_index("survey")
    chips = n_survey // 2
    slots = blocks.shape[0]
    owned = model_hbm.shape[0]
    here = pl.ds(m * owned, owned)
    barrier = pltpu.get_barrier_semaphore()
    for j in range(1, n_mp):
        pl.semaphore_signal(
            barrier, inc=1, device_id=((m + j) % n_mp, s), device_id_type=MESH
        )
    smalls = [
        pltpu.make_async_copy(count_hbm, count_ref, small_sem.at[0]),
        pltpu.make_async_copy(rows_hbm, ids_ref.at[0], small_sem.at[1]),
        pltpu.make_async_copy(cols_hbm, ids_ref.at[1], small_sem.at[2]),
        pltpu.make_async_copy(model_hbm, slab.at[here], small_sem.at[3]),
    ]
    part = slots // PARTS
    loads = [
        pltpu.make_async_copy(
            sens_hbm.at[0, pl.ds(i * part, part)], blocks.at[pl.ds(i * part, part)], load_sem.at[i]
        )
        for i in range(PARTS)
    ]
    for load in smalls + loads:
        load.start()
    for small in smalls[:3]:
        small.wait()
    count = count_ref[0, 0]
    for base, which in ((ROW, 0), (COL, 1)):
        ids = ids_ref[which]
        if base == ROW:
            owner = ids // per
            ids = (owner % 2 * chips + owner // 2) * per + ids % per
        before, last = link_tables(ids, count)
        tables[pl.ds(base, 1)] = ids
        tables[pl.ds(base + 1, 1)] = before
        tables[pl.ds(base + 2, 1)] = last
    to_scalars = pltpu.make_async_copy(tables, table, small_sem.at[4])
    to_scalars.start()
    if n_mp > 1:
        pl.semaphore_wait(barrier, n_mp - 1)
    sends = [
        copy(model_hbm, slab.at[here], model_sem, j - 1, ((m + j) % n_mp, s))
        for j in range(1, n_mp)
    ]
    for send in sends:
        send.start()
    for load in loads + [to_scalars, smalls[3]]:
        load.wait()
    for send in sends:
        send.wait()


def kernel(
    n_mp, n_survey, table, slab, blocks, model_ref, seen_ref, weight_ref, out_ref,
    chain, sib_send, sib_recv, chip_send, chip_recv, resid, grad_send, grad_recv,
    sib_sem, chip_sem, gather_sem, relay_sem, grad_sem,
):
    m = lax.axis_index("mp")
    s = lax.axis_index("survey")
    chips = n_survey // 2
    chip, core = s // 2, s % 2
    sibling = (m, chip * 2 + 1 - core)
    slots = blocks.shape[0]
    owned = model_ref.shape[0]
    per = seen_ref.shape[0]

    def chip_at(j):
        return (chip + j) % chips

    barrier = pltpu.get_barrier_semaphore()
    partners = [((m + j) % n_mp, s) for j in range(1, n_mp)] + [sibling]
    partners += [(m, chip_at(j) * 2 + core) for j in range(1, chips)]
    for partner in partners:
        pl.semaphore_signal(barrier, inc=1, device_id=partner, device_id_type=MESH)
    for i in range(owned):
        out_ref[i] = smoothing(model_ref[i].astype(jnp.float32))
    chain[0] = jnp.zeros(chain.shape[1:], jnp.float32)

    def forward():
        def body(g, carry):
            base = g * UNROLL
            terms = [
                lax.dot_general(
                    slab[table[COL, base + u]],
                    blocks[base + u],
                    (((1,), (1,)), ((), ())),
                    preferred_element_type=jnp.float32,
                )
                for u in range(UNROLL)
            ]
            for u in range(UNROLL):
                before = chain[table[ROW_BEFORE, base + u]]
                chain[base + u + 1] = terms[u] + before
            return carry

        lax.fori_loop(0, slots // UNROLL, body, 0)

    def backward():
        def body(g, carry):
            base = g * UNROLL
            terms = [
                jnp.dot(
                    resid[table[ROW, base + u]],
                    blocks[base + u],
                    preferred_element_type=jnp.float32,
                )
                for u in range(UNROLL)
            ]
            for u in range(UNROLL):
                before = chain[table[COL_BEFORE, base + u]]
                chain[base + u + 1] = terms[u] + before
            return carry

        lax.fori_loop(0, slots // UNROLL, body, 0)

    forward()
    pl.semaphore_wait(barrier, len(partners))

    order = list(range(1, chips)) + [0]
    group = chips // SWAPS
    swaps, scatters, gathers, returns = {}, {}, {}, {}
    for p, j in enumerate(order):
        for i in range(per):
            row = ((1 - core) * chips + chip_at(j)) * per + i
            sib_send[p, i] = chain[table[ROW_LAST, row]]
        if (p + 1) % group == 0:
            some = pl.ds(p + 1 - group, group)
            swaps[p] = copy(sib_send.at[some], sib_recv.at[some], sib_sem, p, sibling)
            swaps[p].start()
    for p, j in enumerate(order):
        if p % group == 0:
            swaps[p + group - 1].wait_recv()
        for i in range(per):
            row = (core * chips + chip_at(j)) * per + i
            chip_send[j, i] = chain[table[ROW_LAST, row]] + sib_recv[p, i]
        if j:
            scatters[j] = copy(
                chip_send.at[j], chip_recv.at[j], chip_sem, j, (m, chip_at(j) * 2 + core)
            )
            scatters[j].start()

    total = chip_send[0]
    for j in range(1, chips):
        scatters[j].wait_recv()
        total += chip_recv[j]
    value = weight_ref[...].astype(jnp.float32) * (total - seen_ref[...].astype(jnp.float32))
    here = pl.ds((core * chips + chip) * per, per)
    resid[here] = value.astype(jnp.bfloat16)
    for j in range(1, chips):
        gathers[j] = copy(
            resid.at[here], resid.at[here], gather_sem, j, (m, chip_at(j) * 2 + core)
        )
        gathers[j].start()
    for j in range(1, chips):
        gathers[j].wait_recv()
    same = resid.at[pl.ds(core * chips * per, chips * per)]
    relay = copy(same, same, relay_sem, 0, sibling)
    relay.start()
    relay.wait_recv()

    backward()

    for j in range(1, n_mp):
        owner = (m + j) % n_mp
        for i in range(owned):
            grad_send[j, i] = chain[table[COL_LAST, owner * owned + i]]
        returns[j] = copy(grad_send.at[j], grad_recv.at[j], grad_sem, j, (owner, s))
        returns[j].start()
    for i in range(owned):
        out_ref[i] += chain[table[COL_LAST, m * owned + i]]
    for j in range(1, n_mp):
        returns[j].wait_recv()
        out_ref[...] += grad_recv[j]

    relay.wait_send()
    for sent in (swaps, scatters, gathers, returns):
        for one in sent.values():
            one.wait_send()


def on_device(
    n_mp, n_survey, model, observed, weights, sensitivity, block_rows, block_cols, block_count
):
    slots = block_rows.shape[1]
    owned, steps, cells = model.shape
    per = observed.shape[0]
    chips = n_survey // 2
    pair = lambda n: pltpu.SemaphoreType.DMA((2, n))
    f32, bf16, i32 = jnp.float32, jnp.bfloat16, jnp.int32
    hbm = pl.BlockSpec(memory_space=pl.ANY)
    smem = pl.BlockSpec(memory_space=pltpu.SMEM)
    vmem = pl.BlockSpec(memory_space=pltpu.VMEM)
    keep = lambda x: pltpu.with_memory_space_constraint(x, pltpu.HBM)
    share = pltpu.VMEM((chips, per, steps, cells), f32)
    table, slab, blocks = pl.pallas_call(
        functools.partial(collect, n_mp, n_survey, per),
        out_shape=[
            jax.ShapeDtypeStruct((8, slots), i32),
            jax.ShapeDtypeStruct((owned * n_mp, steps, cells), bf16),
            jax.ShapeDtypeStruct(sensitivity.shape[1:], bf16),
        ],
        in_specs=[hbm] * 5,
        out_specs=[smem, vmem, vmem],
        scratch_shapes=[
            pltpu.VMEM((2, 1, slots), i32),
            pltpu.SMEM((1, 1), i32),
            pltpu.VMEM((8, slots), i32),
            pltpu.SemaphoreType.DMA((PARTS,)),
            pltpu.SemaphoreType.DMA((5,)),
            pair(n_mp),
        ],
        compiler_params=pltpu.CompilerParams(
            collective_id=0, has_side_effects=True, vmem_limit_bytes=LIMIT << 20
        ),
    )(keep(block_rows), keep(block_cols), block_count, keep(model), keep(sensitivity))
    return pl.pallas_call(
        functools.partial(kernel, n_mp, n_survey),
        out_shape=jax.ShapeDtypeStruct(model.shape, f32),
        in_specs=[smem] + [vmem] * 5,
        out_specs=vmem,
        scratch_shapes=[
            pltpu.VMEM((slots + 1, steps, cells), f32),
            share,
            share,
            share,
            share,
            pltpu.VMEM((per * n_survey, steps, cells), bf16),
            pltpu.VMEM((n_mp, owned, steps, cells), f32),
            pltpu.VMEM((n_mp, owned, steps, cells), f32),
            pair(chips),
            pair(chips),
            pair(chips),
            pair(chips),
            pair(n_mp),
        ],
        compiler_params=pltpu.CompilerParams(
            collective_id=1, has_side_effects=True, vmem_limit_bytes=LIMIT << 20
        ),
    )(table, slab, blocks, model, observed, weights)


def solution(mesh):
    n_mp, n_survey = mesh.shape["mp"], mesh.shape["survey"]
    in_specs = (
        P(("mp", "survey"), None, None),
        P(("mp", "survey"), None, None),
        P(("mp", "survey"), None, None),
        P("mp", "survey", None, None),
        P("mp", "survey"),
        P("mp", "survey"),
        P("mp", "survey"),
    )
    out_specs = P(("mp", "survey"), None, None)
    return jax.shard_map(
        functools.partial(on_device, n_mp, n_survey),
        mesh=mesh,
        in_specs=in_specs,
        out_specs=out_specs,
        check_vma=False,
    )
```
